128 devices in a mesh: seq: 16 (over z, y_lo, core), section: 8 (over x, y_hi).
Axes of the slice: x: 4, y: 4 (y_hi: 2, y_lo: 2; y = y_hi * 2 + y_lo), z: 4, core: 2. Of those that a mesh axis runs over, the one named last changes fastest.
Arguments:
- query: bfloat16 [8, 6144, 3072], P('section', 'seq'), may hold values from -24 to 24, as said below
- key: bfloat16 [8, 6144, 3072], P('section', 'seq'), may hold values from -24 to 24
- value: bfloat16 [8, 6144, 3072], P('section', 'seq'), may hold values from -6 to 6
- cotangent: bfloat16 [8, 6144, 3072], P('section', 'seq'), may hold values from -96 to 96
- adjacency: int32 [48, 9], P('seq'), may hold values from 0 to 1, as said below
Outputs:
- gradients: bfloat16 [8, 6144, 3, 3072], P('section', 'seq')
The draws below stay inside these ranges and needn't reach their ends.
Inputs may be any that keep to these rules, and one draw needn't show every extreme that they name: query and key are drawn together. `adjacency`: the tile relation is symmetric: query tile a attends key tile b exactly when query tile b attends key tile a; every tile attends itself.
All inputs are finite; a program needn't handle non-finite values.
Results may differ from the reference program's by a relative error of at most 0.009.
Values may be sent and summed in bfloat16 or wider, within the bound.
A program may use at most 128 MiB of HBM per device.

```python
import jax
import jax.numpy as jnp
from jax import lax

HEADS = 24
HD = 128
TILE = 128
TOK_DEV = 384
TOKENS = 6144
SECTIONS = 8


def pair_draw(key):
    base = jax.random.fold_in(key, 7)
    key_query, key_keys = jax.random.split(base, 2)
    shape = (SECTIONS, TOKENS, HEADS * HD)
    queries = jnp.clip(jax.random.normal(key_query, shape, jnp.float32), -4.0, 4.0)
    keys = jnp.clip(jax.random.normal(key_keys, shape, jnp.float32), -4.0, 4.0)
    return (queries.astype(jnp.bfloat16), keys.astype(jnp.bfloat16))


def draw_query(key, part):
    return pair_draw(key)[0]


def draw_key(key, part):
    return pair_draw(key)[1]


def draw_adjacency(key, part):
    tiles = TOKENS // TILE
    per_shard = TOK_DEV // TILE
    shards = TOKENS // TOK_DEV
    key_level, key_coin = jax.random.split(jax.random.fold_in(key, 13))
    levels = jax.random.randint(key_level, (tiles,), 1, 5)
    coins = jax.random.randint(key_coin, (tiles, tiles), 0, 8)
    rows = jnp.arange(tiles)[:, None]
    cols = jnp.arange(tiles)[None, :]
    coins = jnp.where(rows < cols, coins, coins.T)
    links = (coins < levels[:, None] + levels[None, :]) | (rows == cols)
    slots = jnp.arange(3 * per_shard)[None, :]
    target = (rows // per_shard + slots // per_shard - 1) % shards * per_shard + slots % per_shard
    return jnp.take_along_axis(links, target, axis=1).astype(jnp.int32)


def steps_of(stream_key, extent, cuts, low, top_value):
    factor_of = 1.0
    for axis_at, blocks in cuts:
        steps = jax.random.uniform(jax.random.fold_in(jax.random.fold_in(stream_key, 6), axis_at), (blocks,), jnp.float32, low / len(cuts), top_value / len(cuts))
        factor_of = factor_of * jnp.repeat(jnp.exp(steps), extent[axis_at] // blocks).reshape((-1,) + (1,) * (len(extent) - 1 - axis_at))
    return factor_of


def centred(key, dims, spread, limit, cuts=(), dtype=jnp.bfloat16):
    loudness = steps_of(key, dims, cuts, -0.22, 0.18) if cuts else 1.0
    entries = jax.random.normal(key, dims, jnp.float32) * spread * loudness
    return jnp.minimum(jnp.maximum(entries, -limit), limit).astype(dtype)


def setup_inputs(seed: int = 0) -> dict:
    seeds = jax.random.split(jax.random.key(seed), 6)
    return {
        "query": draw_query(jax.random.fold_in(seeds[5], 71), 0),
        "key": draw_key(jax.random.fold_in(seeds[5], 71), 0),
        "value": centred(seeds[2], (SECTIONS, TOKENS, HEADS * HD), 1.0, 6.0, ((0, 8), (1, 16))),
        "cotangent": centred(seeds[3], (SECTIONS, TOKENS, HEADS * HD), 16.0, 96.0, ((0, 8), (1, 16))),
        "adjacency": draw_adjacency(jax.random.fold_in(seeds[5], 71), 0),
    }


def shard_terms(queries, keys, values, cotangent, mask):
    scale = HD ** -0.5
    q_full = queries.astype(jnp.float32)
    k_full = keys.astype(jnp.float32)
    v_full = values.astype(jnp.float32)
    o_full = cotangent.astype(jnp.float32)
    scores = jnp.einsum("rhc,khc->hrk", q_full, k_full) * scale
    scores = jnp.where(mask[None], scores, -jnp.inf)
    top = jnp.max(scores, axis=2)
    weight = jnp.exp(scores - top[:, :, None])
    total = jnp.sum(weight, axis=2)
    prob = weight / total[:, :, None]
    prob_half = lax.optimization_barrier(prob.astype(jnp.bfloat16)).astype(jnp.float32)
    output = jnp.einsum("hrk,khc->rhc", prob_half, v_full)
    delta = jnp.einsum("rhc,rhc->hr", o_full, output)
    dprob = jnp.einsum("rhc,khc->hrk", o_full, v_full)
    dscore = lax.optimization_barrier((prob * (dprob - delta[:, :, None])).astype(jnp.bfloat16)).astype(jnp.float32)
    grad_query = jnp.einsum("hrk,khc->rhc", dscore, k_full) * scale
    part_key = jnp.einsum("hrk,rhc->khc", dscore, q_full) * scale
    part_value = jnp.einsum("hrk,rhc->khc", prob_half, o_full)
    return grad_query.astype(jnp.bfloat16), part_key.astype(jnp.bfloat16), part_value.astype(jnp.bfloat16)


def reference(query, key, value, cotangent, adjacency):
    shards = TOKENS // TOK_DEV
    per_shard = TOK_DEV // TILE
    full_width = HEADS * HD
    blocks = adjacency.reshape(shards, per_shard, 3 * per_shard)
    masks = jnp.broadcast_to(blocks[:, :, None, :, None] > 0, (shards, per_shard, TILE, 3 * per_shard, TILE))
    masks = masks.reshape(shards, TOK_DEV, 3 * TOK_DEV)

    def owners(part):
        part = part.astype(jnp.float32).reshape(shards, 3, TOK_DEV, full_width)
        summed = jnp.roll(part[:, 0], -1, 0) + part[:, 1] + jnp.roll(part[:, 2], 1, 0)
        return summed.astype(jnp.bfloat16).reshape(TOKENS, full_width)

    results = []
    for section in range(SECTIONS):
        queries = query[section].reshape(shards, TOK_DEV, HEADS, HD)
        keys = key[section].reshape(shards, TOK_DEV, HEADS, HD)
        values = value[section].reshape(shards, TOK_DEV, HEADS, HD)
        grads_out = cotangent[section].reshape(shards, TOK_DEV, HEADS, HD)
        window_keys = jnp.concatenate([jnp.roll(keys, 1, 0), keys, jnp.roll(keys, -1, 0)], axis=1)
        window_values = jnp.concatenate([jnp.roll(values, 1, 0), values, jnp.roll(values, -1, 0)], axis=1)
        grad_query, part_key, part_value = lax.map(
            lambda items: shard_terms(items[0], items[1], items[2], items[3], items[4]),
            (queries, window_keys, window_values, grads_out, masks))
        stacked = jnp.stack([grad_query.reshape(TOKENS, full_width), owners(part_key), owners(part_value)], axis=1)
        results.append(stacked)
    gathered = jnp.stack(results, 0)
    return jnp.roll(gathered, -1, 0)
```

```python
import functools
import math

import jax
import jax.numpy as jnp
from jax import lax
from jax.experimental import pallas as pl
from jax.experimental.pallas import tpu as pltpu
from jax.sharding import PartitionSpec as P

HD = 128
QUAD = 4
NEG = -1e30
BF = jnp.bfloat16
F32 = jnp.float32


def dot(a, b, dims):
    return lax.dot_general(a, b, (dims, ((), ())), preferred_element_type=F32)


def kernel(
    q_ref, k_ref, v_ref, o_ref, bias_ref, out_ref,
    kvb, qob, biasb, ob, hs, hr, rl, acc,
    r_kv, r_qo, r_b, r_halo, r_part, r_rl, r_fin,
    s_in, s_b, s_halo, s_part, s_out, s_rl,
    *, rows, own, tile, sections, shards,
):
    nz = shards // QUAD
    seq = lax.axis_index("seq")
    sec = lax.axis_index("section")
    z, g = seq // QUAD, seq % QUAD
    p, c = g // 2, g % 2
    base = z * QUAD
    target = (sec + sections - 1) % sections
    source = (sec + 1) % sections
    other = base + 2 * (1 - p)
    z_prev = ((z + nz - 1) % nz) * QUAD + g
    z_next = ((z + 1) % nz) * QUAD + g
    scale = HD**-0.5
    window = 3 * rows
    mesh_id = pl.DeviceIdType.MESH

    def device(at_seq, at_sec=None):
        return {"seq": at_seq, "section": sec if at_sec is None else at_sec}

    def cols(head):
        return pl.ds(pl.multiple_of(head * HD, HD), HD)

    def slab(slot):
        return pl.ds(pl.multiple_of(slot * rows, rows), rows)

    def send(src, dst, ssem, rsem, to):
        pltpu.make_async_remote_copy(
            src_ref=src, dst_ref=dst, send_sem=ssem, recv_sem=rsem, device_id=to, device_id_type=mesh_id
        ).start()

    def wait(ref, sem):
        pltpu.make_async_copy(ref, ref, sem).wait()

    barrier = pltpu.get_barrier_semaphore()
    partners = [device(base + (g + d) % QUAD) for d in range(1, QUAD)]
    partners += [device(z_prev), device(z_next)]
    partners += [device(other + e, target) for e in range(2)]
    partners += [device(other + e, source) for e in range(2)]
    for to in partners:
        pl.semaphore_signal(barrier, inc=1, device_id=to, device_id_type=mesh_id)
    pl.semaphore_wait(barrier, len(partners))

    for d in range(1, QUAD):
        to = device(base + (g + d) % QUAD)
        send(bias_ref, biasb.at[g], s_b.at[d - 1], r_b.at[g], to)
    pltpu.make_async_copy(bias_ref, biasb.at[g], r_b.at[g]).start()

    def scatter(h, carry):
        mine = cols(g * own + h)
        pltpu.make_async_copy(k_ref.at[:, mine], kvb.at[h, 0, slab(g + 1)], r_kv.at[h, g]).start()
        pltpu.make_async_copy(v_ref.at[:, mine], kvb.at[h, 1, slab(g + 1)], r_kv.at[h, g]).start()
        pltpu.make_async_copy(q_ref.at[:, mine], qob.at[h, 0, slab(g)], r_qo.at[h, g]).start()
        pltpu.make_async_copy(o_ref.at[:, mine], qob.at[h, 1, slab(g)], r_qo.at[h, g]).start()
        for d in (2, 3, 1):
            peer = (g + d) % QUAD
            to = device(base + peer)
            theirs = cols(peer * own + h)
            send(k_ref.at[:, theirs], kvb.at[h, 0, slab(g + 1)], s_in.at[h], r_kv.at[h, g], to)
            send(v_ref.at[:, theirs], kvb.at[h, 1, slab(g + 1)], s_in.at[h], r_kv.at[h, g], to)
        for d in (2, 3, 1):
            peer = (g + d) % QUAD
            to = device(base + peer)
            theirs = cols(peer * own + h)
            send(q_ref.at[:, theirs], qob.at[h, 0, slab(g)], s_in.at[h], r_qo.at[h, g], to)
            send(o_ref.at[:, theirs], qob.at[h, 1, slab(g)], s_in.at[h], r_qo.at[h, g], to)
        return carry

    lax.fori_loop(0, own, scatter, 0)

    def post(h, i, first, count, kind):
        to = device(other + i % 2, target)
        src = ob.at[h, i, pl.ds(first, count)]

        @pl.when(i // 2 != p)
        def _():
            send(src, out_ref.at[pl.ds(first, count), :, cols(g * own + h)], s_out.at[h], r_fin.at[h], to)

        @pl.when(i // 2 == p)
        def _():
            send(src, rl.at[h, c, pl.ds(first, count)], s_out.at[h], r_rl.at[h, c, kind], to)

    def relay(h):
        to = device(other + c)
        for kind, first, count in ((0, 0, 1), (1, 1, 2)):
            for e in range(2):
                block = rl.at[h, e, pl.ds(first, count)]
                wait(block, r_rl.at[h, e, kind])
                head = (2 * (1 - p) + e) * own + h
                send(block, out_ref.at[pl.ds(first, count), :, cols(head)], s_rl.at[h], r_fin.at[h], to)

    def attend(h, i):
        win = pl.ds(pl.multiple_of(i * rows, rows), window)
        keys, values = kvb[h, 0, win, :], kvb[h, 1, win, :]
        queries, grads = qob[h, 0, slab(i), :], qob[h, 1, slab(i), :]
        scores = dot(keys, queries, ((1,), (1,)))
        bias = biasb[i]
        count = window // tile
        scores = jnp.concatenate(
            [scores[j * tile : (j + 1) * tile] + bias[j : j + 1] for j in range(count)], axis=0
        )
        top = jnp.max(scores, axis=0, keepdims=True)
        weight = jnp.exp2((scores - top) * (scale * math.log2(math.e)))
        total = jnp.sum(weight, axis=0, keepdims=True)
        prob = weight * (1.0 / total)
        half = prob.astype(BF)
        dprob = dot(values, grads, ((1,), (1,)))
        delta = jnp.sum(half.astype(F32) * dprob, axis=0, keepdims=True)
        dscore = (prob * (dprob - delta)).astype(BF)
        ob[h, i, 0] = (dot(dscore, keys, ((0,), (0,))) * scale).astype(BF)
        acc[0, win, :] += dot(dscore, queries, ((1,), (0,)))
        acc[1, win, :] += dot(half, grads, ((1,), (0,)))

    for e in range(QUAD):
        wait(bias_ref, r_b.at[e])

    def step(h, carry):
        kv_slot = lambda slot: kvb.at[h, :, slab(slot)]
        wait(kv_slot(1), r_kv.at[h, 0])
        send(kv_slot(1), kv_slot(QUAD + 1), s_halo.at[h, 0], r_halo.at[h, 1], device(z_prev))
        wait(kv_slot(QUAD), r_kv.at[h, QUAD - 1])
        send(kv_slot(QUAD), kv_slot(0), s_halo.at[h, 1], r_halo.at[h, 0], device(z_next))
        acc[...] = jnp.zeros_like(acc)
        for e in range(1, QUAD - 1):
            wait(kv_slot(e + 1), r_kv.at[h, e])
        for e in range(QUAD):
            wait(qob.at[h, :, slab(e)], r_qo.at[h, e])
        wait(kv_slot(0), r_halo.at[h, 0])
        wait(kv_slot(QUAD + 1), r_halo.at[h, 1])

        def query_slot(index, inner):
            i = (3 * index) % QUAD
            attend(h, i)
            post(h, i, 0, 1, 0)

            @pl.when(index == 0)
            def _():
                hs[h, 0, 0] = (acc[0, 0:rows] * scale).astype(BF)
                hs[h, 0, 1] = acc[1, 0:rows].astype(BF)
                send(hs.at[h, 0], hr.at[h, 1], s_part.at[h, 0], r_part.at[h, 1], device(z_prev))

            @pl.when(index == 1)
            def _():
                hs[h, 1, 0] = (acc[0, 5 * rows :] * scale).astype(BF)
                hs[h, 1, 1] = acc[1, 5 * rows :].astype(BF)
                send(hs.at[h, 1], hr.at[h, 0], s_part.at[h, 1], r_part.at[h, 0], device(z_next))

            return inner

        lax.fori_loop(0, QUAD, query_slot, 0)
        for i in (1, 2):
            ob[h, i, 1] = (acc[0, (i + 1) * rows : (i + 2) * rows] * scale).astype(BF)
            ob[h, i, 2] = acc[1, (i + 1) * rows : (i + 2) * rows].astype(BF)
            post(h, jnp.int32(i), 1, 2, 1)
        for side, i in ((0, 0), (1, QUAD - 1)):
            wait(hr.at[h, side], r_part.at[h, side])
            ob[h, i, 1] = (
                acc[0, (i + 1) * rows : (i + 2) * rows] * scale + hr[h, side, 0].astype(F32)
            ).astype(BF)
            ob[h, i, 2] = (acc[1, (i + 1) * rows : (i + 2) * rows] + hr[h, side, 1].astype(F32)).astype(BF)
            post(h, jnp.int32(i), 1, 2, 1)

        @pl.when(h >= LAG)
        def _():
            relay(h - LAG)

        return carry

    lax.fori_loop(0, own, step, 0)

    def tail(h, carry):
        relay(h)
        return carry

    lax.fori_loop(max(own - LAG, 0), own, tail, 0)

    def drain(h, carry):
        wait(ob.at[h], s_in.at[h])
        wait(ob.at[h], s_out.at[h])
        wait(rl.at[h], s_rl.at[h])
        for e in range(2):
            wait(hs.at[h, e], s_halo.at[h, e])
            wait(hs.at[h, e], s_part.at[h, e])
        wait(ob.at[h], r_fin.at[h])
        return carry

    lax.fori_loop(0, own, drain, 0)
    for d in range(QUAD - 1):
        wait(bias_ref, s_b.at[d])


LAG = 2


def per_device(query, key, value, cotangent, adjacency, *, sections, shards):
    _, rows, width = query.shape
    own = width // HD // QUAD
    tiles, links = adjacency.shape
    tile = rows // tiles
    bias = jnp.where(adjacency > 0, 0.0, NEG).astype(F32).T
    bias = jnp.repeat(bias, tile, axis=1)
    bias = jnp.pad(bias, ((0, 16 - links), (0, 0)))
    dma, vmem = pltpu.SemaphoreType.DMA, pltpu.VMEM
    hbm = pl.BlockSpec(memory_space=pltpu.HBM)
    out = pl.pallas_call(
        functools.partial(kernel, rows=rows, own=own, tile=tile, sections=sections, shards=shards),
        out_shape=jax.ShapeDtypeStruct((3, rows, width), BF),
        in_specs=[hbm] * 5,
        out_specs=pl.BlockSpec(memory_space=pl.ANY),
        scratch_shapes=[
            vmem((own, 2, (QUAD + 2) * rows, HD), BF),
            vmem((own, 2, QUAD * rows, HD), BF),
            vmem((QUAD, 16, rows), F32),
            vmem((own, QUAD, 3, rows, HD), BF),
            vmem((own, 2, 2, rows, HD), BF),
            vmem((own, 2, 2, rows, HD), BF),
            vmem((own, 2, 3, rows, HD), BF),
            vmem((2, (QUAD + 2) * rows, HD), F32),
            dma((own, QUAD)),
            dma((own, QUAD)),
            dma((QUAD,)),
            dma((own, 2)),
            dma((own, 2)),
            dma((own, 2, 2)),
            dma((own,)),
            dma((own,)),
            dma((QUAD - 1,)),
            dma((own, 2)),
            dma((own, 2)),
            dma((own,)),
            dma((own,)),
        ],
        compiler_params=pltpu.CompilerParams(
            collective_id=0, has_side_effects=True, vmem_limit_bytes=52 * 1024 * 1024
        ),
    )(query[0], key[0], value[0], cotangent[0], bias)
    return jnp.transpose(out, (1, 0, 2))[None]


def solution(mesh):
    in_specs = (
        P("section", "seq", None),
        P("section", "seq", None),
        P("section", "seq", None),
        P("section", "seq", None),
        P("seq", None),
    )
    out_specs = P("section", "seq", None, None)
    body = functools.partial(per_device, sections=mesh.shape["section"], shards=mesh.shape["seq"])
    return jax.shard_map(body, mesh=mesh, in_specs=in_specs, out_specs=out_specs, check_vma=False)
```

```python
import functools
import math

import jax
import jax.numpy as jnp
from jax import lax
from jax.experimental import pallas as pl
from jax.experimental.pallas import tpu as pltpu
from jax.sharding import PartitionSpec as P

HD = 128
QUAD = 4
NEG = -1e30
BF = jnp.bfloat16
F32 = jnp.float32


def dot(a, b, dims):
    return lax.dot_general(a, b, (dims, ((), ())), preferred_element_type=F32)


def kernel(
    q_ref, k_ref, v_ref, o_ref, bias_ref, out_ref,
    kvb, qob, rawb, biasb, ob, hs, hr, rl, acc,
    r_kv, r_qo, r_b, r_halo, r_part, r_rl, r_fin,
    s_in, s_b, s_halo, s_part, s_out, s_rl,
    *, rows, own, tile, sections, shards,
):
    nz = shards // QUAD
    seq = lax.axis_index("seq")
    sec = lax.axis_index("section")
    z, g = seq // QUAD, seq % QUAD
    p, c = g // 2, g % 2
    base = z * QUAD
    target = (sec + sections - 1) % sections
    source = (sec + 1) % sections
    other = base + 2 * (1 - p)
    z_prev = ((z + nz - 1) % nz) * QUAD + g
    z_next = ((z + 1) % nz) * QUAD + g
    scale = HD**-0.5
    window = 3 * rows
    mesh_id = pl.DeviceIdType.MESH

    def device(at_seq, at_sec=None):
        return {"seq": at_seq, "section": sec if at_sec is None else at_sec}

    def cols(head):
        return pl.ds(pl.multiple_of(head * HD, HD), HD)

    def slab(slot):
        return pl.ds(pl.multiple_of(slot * rows, rows), rows)

    def send(src, dst, ssem, rsem, to):
        pltpu.make_async_remote_copy(
            src_ref=src, dst_ref=dst, send_sem=ssem, recv_sem=rsem, device_id=to, device_id_type=mesh_id
        ).start()

    def wait(ref, sem):
        pltpu.make_async_copy(ref, ref, sem).wait()

    barrier = pltpu.get_barrier_semaphore()
    partners = [device(base + (g + d) % QUAD) for d in range(1, QUAD)]
    partners += [device(z_prev), device(z_next)]
    partners += [device(other + e, target) for e in range(2)]
    partners += [device(other + e, source) for e in range(2)]
    for to in partners:
        pl.semaphore_signal(barrier, inc=1, device_id=to, device_id_type=mesh_id)
    pl.semaphore_wait(barrier, len(partners))

    for d in range(1, QUAD):
        to = device(base + (g + d) % QUAD)
        send(bias_ref, rawb.at[g], s_b.at[d - 1], r_b.at[g], to)
    pltpu.make_async_copy(bias_ref, rawb.at[g], r_b.at[g]).start()

    def scatter(h, carry):
        mine = cols(g * own + h)
        pltpu.make_async_copy(k_ref.at[:, mine], kvb.at[h, 0, slab(g + 1)], r_kv.at[h, g]).start()
        pltpu.make_async_copy(v_ref.at[:, mine], kvb.at[h, 1, slab(g + 1)], r_kv.at[h, g]).start()
        pltpu.make_async_copy(q_ref.at[:, mine], qob.at[h, 0, slab(g)], r_qo.at[h, g]).start()
        pltpu.make_async_copy(o_ref.at[:, mine], qob.at[h, 1, slab(g)], r_qo.at[h, g]).start()
        for peer in (2 * (1 - p), 2 * (1 - p) + 1, 2 * p + 1 - c):
            to = device(base + peer)
            theirs = cols(peer * own + h)
            send(k_ref.at[:, theirs], kvb.at[h, 0, slab(g + 1)], s_in.at[h], r_kv.at[h, g], to)
            send(v_ref.at[:, theirs], kvb.at[h, 1, slab(g + 1)], s_in.at[h], r_kv.at[h, g], to)
            send(q_ref.at[:, theirs], qob.at[h, 0, slab(g)], s_in.at[h], r_qo.at[h, g], to)
            send(o_ref.at[:, theirs], qob.at[h, 1, slab(g)], s_in.at[h], r_qo.at[h, g], to)
        return carry

    lax.fori_loop(0, own, scatter, 0)

    def post(h, i, first, count, kind):
        to = device(other + i % 2, target)
        src = ob.at[h, i, pl.ds(first, count)]

        @pl.when(i // 2 != p)
        def _():
            send(src, out_ref.at[pl.ds(first, count), :, cols(g * own + h)], s_out.at[h], r_fin.at[h], to)

        @pl.when(i // 2 == p)
        def _():
            send(src, rl.at[h, c, pl.ds(first, count)], s_out.at[h], r_rl.at[h, c, kind], to)

    def relay(h):
        to = device(other + c)
        for kind, first, count in ((0, 0, 1), (1, 1, 2)):
            for e in range(2):
                block = rl.at[h, e, pl.ds(first, count)]
                wait(block, r_rl.at[h, e, kind])
                head = (2 * (1 - p) + e) * own + h
                send(block, out_ref.at[pl.ds(first, count), :, cols(head)], s_rl.at[h], r_fin.at[h], to)

    def attend(h, i):
        win = pl.ds(pl.multiple_of(i * rows, rows), window)
        keys, values = kvb[h, 0, win, :], kvb[h, 1, win, :]
        queries, grads = qob[h, 0, slab(i), :], qob[h, 1, slab(i), :]
        scores = dot(keys, queries, ((1,), (1,)))
        bias = biasb[i]
        count = window // tile
        scores = jnp.concatenate(
            [scores[j * tile : (j + 1) * tile] + bias[j : j + 1] for j in range(count)], axis=0
        )
        top = jnp.max(scores, axis=0, keepdims=True)
        weight = jnp.exp2((scores - top) * (scale * math.log2(math.e)))
        total = jnp.sum(weight, axis=0, keepdims=True)
        prob = weight * (1.0 / total)
        half = prob.astype(BF)
        dprob = dot(values, grads, ((1,), (1,)))
        delta = jnp.sum(half.astype(F32) * dprob, axis=0, keepdims=True)
        dscore = (prob * (dprob - delta)).astype(BF)
        ob[h, i, 0] = (dot(dscore, keys, ((0,), (0,))) * scale).astype(BF)
        acc[0, win, :] += dot(dscore, queries, ((1,), (0,)))
        acc[1, win, :] += dot(half, grads, ((1,), (0,)))

    for e in range(QUAD):
        wait(bias_ref, r_b.at[e])
        rule = rawb[e]
        for j in range(window // tile):
            for n in range(rows // tile):
                biasb[e, j : j + 1, n * tile : (n + 1) * tile] = jnp.broadcast_to(
                    rule[n : n + 1, j : j + 1], (1, tile)
                )

    def step(h, carry):
        kv_slot = lambda slot: kvb.at[h, :, slab(slot)]
        wait(kv_slot(1), r_kv.at[h, 0])
        send(kv_slot(1), kv_slot(QUAD + 1), s_halo.at[h, 0], r_halo.at[h, 1], device(z_prev))
        wait(kv_slot(QUAD), r_kv.at[h, QUAD - 1])
        send(kv_slot(QUAD), kv_slot(0), s_halo.at[h, 1], r_halo.at[h, 0], device(z_next))
        acc[...] = jnp.zeros_like(acc)
        for e in range(1, QUAD - 1):
            wait(kv_slot(e + 1), r_kv.at[h, e])

        def query_slot(index, inner):
            half = index // 2
            first = (1 - index) * (1 - half) + (5 - index) * half
            i = first + p * (QUAD - 1 - 2 * first)
            wait(qob.at[h, :, slab(i)], r_qo.at[h, i])

            @pl.when(i == 0)
            def _():
                wait(kv_slot(0), r_halo.at[h, 0])

            @pl.when(i == QUAD - 1)
            def _():
                wait(kv_slot(QUAD + 1), r_halo.at[h, 1])

            attend(h, i)
            post(h, i, 0, 1, 0)

            @pl.when(i == 0)
            def _():
                hs[h, 0, 0] = (acc[0, 0:rows] * scale).astype(BF)
                hs[h, 0, 1] = acc[1, 0:rows].astype(BF)
                send(hs.at[h, 0], hr.at[h, 1], s_part.at[h, 0], r_part.at[h, 1], device(z_prev))

            @pl.when(i == QUAD - 1)
            def _():
                hs[h, 1, 0] = (acc[0, 5 * rows :] * scale).astype(BF)
                hs[h, 1, 1] = acc[1, 5 * rows :].astype(BF)
                send(hs.at[h, 1], hr.at[h, 0], s_part.at[h, 1], r_part.at[h, 0], device(z_next))

            return inner

        lax.fori_loop(0, QUAD, query_slot, 0)

        def finish(index, inner):
            half = index // 2
            first = (1 - index) * (1 - half) + index * half
            i = first + p * (QUAD - 1 - 2 * first)
            edge = (i == 0) | (i == QUAD - 1)
            side = i // (QUAD - 1)

            @pl.when(edge)
            def _():
                wait(hr.at[h, side], r_part.at[h, side])
                ob[h, i, 1] = (acc[0, slab(i + 1)] * scale + hr[h, side, 0].astype(F32)).astype(BF)
                ob[h, i, 2] = (acc[1, slab(i + 1)] + hr[h, side, 1].astype(F32)).astype(BF)

            @pl.when(jnp.logical_not(edge))
            def _():
                ob[h, i, 1] = (acc[0, slab(i + 1)] * scale).astype(BF)
                ob[h, i, 2] = acc[1, slab(i + 1)].astype(BF)

            post(h, i, 1, 2, 1)
            return inner

        lax.fori_loop(0, QUAD, finish, 0)

        @pl.when(h >= LAG)
        def _():
            relay(h - LAG)

        return carry

    lax.fori_loop(0, own, step, 0)

    def tail(h, carry):
        relay(h)
        return carry

    lax.fori_loop(max(own - LAG, 0), own, tail, 0)

    def drain(h, carry):
        wait(ob.at[h], s_in.at[h])
        wait(ob.at[h], s_out.at[h])
        wait(rl.at[h], s_rl.at[h])
        for e in range(2):
            wait(hs.at[h, e], s_halo.at[h, e])
            wait(hs.at[h, e], s_part.at[h, e])
        wait(ob.at[h], r_fin.at[h])
        return carry

    lax.fori_loop(0, own, drain, 0)
    for d in range(QUAD - 1):
        wait(bias_ref, s_b.at[d])


LAG = 3


def per_device(query, key, value, cotangent, adjacency, *, sections, shards):
    _, rows, width = query.shape
    own = width // HD // QUAD
    tiles, links = adjacency.shape
    tile = rows // tiles
    bias = jnp.where(adjacency > 0, 0.0, NEG).astype(F32)
    bias = jnp.pad(bias, ((0, 8 - tiles), (0, HD - links)))
    dma, vmem = pltpu.SemaphoreType.DMA, pltpu.VMEM
    hbm = pl.BlockSpec(memory_space=pltpu.HBM)
    out = pl.pallas_call(
        functools.partial(kernel, rows=rows, own=own, tile=tile, sections=sections, shards=shards),
        out_shape=pltpu.VMEM((3, rows, width), BF),
        in_specs=[hbm] * 5,
        out_specs=pl.BlockSpec(memory_space=pltpu.VMEM),
        scratch_shapes=[
            vmem((own, 2, (QUAD + 2) * rows, HD), BF),
            vmem((own, 2, QUAD * rows, HD), BF),
            vmem((QUAD, 8, HD), F32),
            vmem((QUAD, 16, rows), F32),
            vmem((own, QUAD, 3, rows, HD), BF),
            vmem((own, 2, 2, rows, HD), BF),
            vmem((own, 2, 2, rows, HD), BF),
            vmem((own, 2, 3, rows, HD), BF),
            vmem((2, (QUAD + 2) * rows, HD), F32),
            dma((own, QUAD)),
            dma((own, QUAD)),
            dma((QUAD,)),
            dma((own, 2)),
            dma((own, 2)),
            dma((own, 2, 2)),
            dma((own,)),
            dma((own,)),
            dma((QUAD - 1,)),
            dma((own, 2)),
            dma((own, 2)),
            dma((own,)),
            dma((own,)),
        ],
        compiler_params=pltpu.CompilerParams(
            collective_id=0, has_side_effects=True, vmem_limit_bytes=54 * 1024 * 1024
        ),
    )(query[0], key[0], value[0], cotangent[0], bias)
    return jnp.transpose(out, (1, 0, 2))[None]


def solution(mesh):
    in_specs = (
        P("section", "seq", None),
        P("section", "seq", None),
        P("section", "seq", None),
        P("section", "seq", None),
        P("seq", None),
    )
    out_specs = P("section", "seq", None, None)
    body = functools.partial(per_device, sections=mesh.shape["section"], shards=mesh.shape["seq"])
    return jax.shard_map(body, mesh=mesh, in_specs=in_specs, out_specs=out_specs, check_vma=False)
```

```python
import functools
import math

import jax
import jax.numpy as jnp
from jax import lax
from jax.experimental import pallas as pl
from jax.experimental.pallas import tpu as pltpu
from jax.sharding import PartitionSpec as P

HD = 128
QUAD = 4
NEG = -1e30
BF = jnp.bfloat16
F32 = jnp.float32


def dot(a, b, dims):
    return lax.dot_general(a, b, (dims, ((), ())), preferred_element_type=F32)


def kernel(
    q_ref, k_ref, v_ref, o_ref, adj_ref, out_ref,
    kvb, qob, adjb, biasb, ob, hs, hr, rl, acc,
    r_kv, r_qo, r_b, r_halo, r_part, r_rl, r_fin,
    s_in, s_b, s_halo, s_part, s_out, s_rl, quad_in, near_in,
    *, rows, own, tile, sections, shards,
):
    nz = shards // QUAD
    seq = lax.axis_index("seq")
    sec = lax.axis_index("section")
    z, g = seq // QUAD, seq % QUAD
    p, c = g // 2, g % 2
    base = z * QUAD
    target = (sec + sections - 1) % sections
    source = (sec + 1) % sections
    other = base + 2 * (1 - p)
    z_prev = ((z + nz - 1) % nz) * QUAD + g
    z_next = ((z + 1) % nz) * QUAD + g
    scale = HD**-0.5
    window = 3 * rows
    mesh_id = pl.DeviceIdType.MESH

    def device(at_seq, at_sec=None):
        return {"seq": at_seq, "section": sec if at_sec is None else at_sec}

    def cols(head):
        return pl.ds(pl.multiple_of(head * HD, HD), HD)

    def slab(slot):
        return pl.ds(pl.multiple_of(slot * rows, rows), rows)

    def send(src, dst, ssem, rsem, to):
        pltpu.make_async_remote_copy(
            src_ref=src, dst_ref=dst, send_sem=ssem, recv_sem=rsem, device_id=to, device_id_type=mesh_id
        ).start()

    def wait(ref, sem):
        pltpu.make_async_copy(ref, ref, sem).wait()

    barrier = pltpu.get_barrier_semaphore()
    for e in (0, 2):

        @pl.when(g != e)
        def _():
            pl.semaphore_signal(barrier, inc=1, device_id=device(base + e), device_id_type=mesh_id)

    @pl.when(c == 0)
    def _():
        pl.semaphore_wait(barrier, QUAD - 1)
        pl.semaphore_signal(quad_in, inc=1, device_id=device(base + g + 1), device_id_type=mesh_id)
        for to in (device(z_prev + 1), device(z_next + 1), device(seq + 1, target), device(seq + 1, source)):
            pl.semaphore_signal(barrier, inc=1, device_id=to, device_id_type=mesh_id)

    @pl.when(c == 1)
    def _():
        pl.semaphore_wait(quad_in, 1)

    for d in range(1, QUAD):
        to = device(base + (g + d) % QUAD)
        send(adj_ref, adjb.at[g], s_b.at[d - 1], r_b.at[g], to)
    pltpu.make_async_copy(adj_ref, adjb.at[g], r_b.at[g]).start()

    def scatter(h, carry):
        mine = cols(g * own + h)
        pltpu.make_async_copy(k_ref.at[:, mine], kvb.at[h, 0, slab(g + 1)], r_kv.at[h, g]).start()
        pltpu.make_async_copy(v_ref.at[:, mine], kvb.at[h, 1, slab(g + 1)], r_kv.at[h, g]).start()
        pltpu.make_async_copy(q_ref.at[:, mine], qob.at[h, 0, slab(g)], r_qo.at[h, g]).start()
        pltpu.make_async_copy(o_ref.at[:, mine], qob.at[h, 1, slab(g)], r_qo.at[h, g]).start()
        for peer in (2 * (1 - p), 2 * (1 - p) + 1, 2 * p + 1 - c):
            to = device(base + peer)
            theirs = cols(peer * own + h)
            send(k_ref.at[:, theirs], kvb.at[h, 0, slab(g + 1)], s_in.at[h], r_kv.at[h, g], to)
            send(v_ref.at[:, theirs], kvb.at[h, 1, slab(g + 1)], s_in.at[h], r_kv.at[h, g], to)
            send(q_ref.at[:, theirs], qob.at[h, 0, slab(g)], s_in.at[h], r_qo.at[h, g], to)
            send(o_ref.at[:, theirs], qob.at[h, 1, slab(g)], s_in.at[h], r_qo.at[h, g], to)
        return carry

    lax.fori_loop(0, own, scatter, 0)

    @pl.when(c == 1)
    def _():
        pl.semaphore_wait(barrier, 4)
        pl.semaphore_signal(near_in, inc=1, device_id=device(base + g - 1), device_id_type=mesh_id)

    @pl.when(c == 0)
    def _():
        pl.semaphore_wait(near_in, 1)


    def post(h, i, first, count, kind):
        to = device(other + i % 2, target)
        src = ob.at[h, i, pl.ds(first, count)]

        @pl.when(i // 2 != p)
        def _():
            send(src, out_ref.at[pl.ds(first, count), :, cols(g * own + h)], s_out.at[h], r_fin.at[h], to)

        @pl.when(i // 2 == p)
        def _():
            send(src, rl.at[h, c, pl.ds(first, count)], s_out.at[h], r_rl.at[h, c, kind], to)

    def relay(h):
        to = device(other + c)
        for kind, first, count in ((0, 0, 1), (1, 1, 2)):
            for e in range(2):
                block = rl.at[h, e, pl.ds(first, count)]
                wait(block, r_rl.at[h, e, kind])
                head = (2 * (1 - p) + e) * own + h
                send(block, out_ref.at[pl.ds(first, count), :, cols(head)], s_rl.at[h], r_fin.at[h], to)

    def attend(h, i):
        win = pl.ds(pl.multiple_of(i * rows, rows), window)
        keys, values = kvb[h, 0, win, :], kvb[h, 1, win, :]
        queries, grads = qob[h, 0, slab(i), :], qob[h, 1, slab(i), :]
        scores = dot(keys, queries, ((1,), (1,)))
        bias = biasb[i]
        count = window // tile
        scores = jnp.concatenate(
            [scores[j * tile : (j + 1) * tile] + bias[j : j + 1] for j in range(count)], axis=0
        )
        top = jnp.max(scores, axis=0, keepdims=True)
        weight = jnp.exp2((scores - top) * (scale * math.log2(math.e)))
        total = jnp.sum(weight, axis=0, keepdims=True)
        prob = weight * (1.0 / total)
        half = prob.astype(BF)
        dprob = dot(values, grads, ((1,), (1,)))
        delta = jnp.sum(half.astype(F32) * dprob, axis=0, keepdims=True)
        dscore = (prob * (dprob - delta)).astype(BF)
        ob[h, i, 0] = (dot(dscore, keys, ((0,), (0,))) * scale).astype(BF)
        acc[0, win, :] += dot(dscore, queries, ((1,), (0,)))
        acc[1, win, :] += dot(half, grads, ((1,), (0,)))

    for e in range(QUAD):
        wait(adj_ref, r_b.at[e])
        rule = adjb[e]
        for j in range(window // tile):
            for n in range(rows // tile):
                link = jnp.broadcast_to(rule[n : n + 1, j : j + 1], (1, tile))
                biasb[e, j : j + 1, n * tile : (n + 1) * tile] = jnp.where(link > 0, 0.0, NEG)

    def step(h, carry):
        kv_slot = lambda slot: kvb.at[h, :, slab(slot)]
        wait(kv_slot(1), r_kv.at[h, 0])
        send(kv_slot(1), kv_slot(QUAD + 1), s_halo.at[h, 0], r_halo.at[h, 1], device(z_prev))
        wait(kv_slot(QUAD), r_kv.at[h, QUAD - 1])
        send(kv_slot(QUAD), kv_slot(0), s_halo.at[h, 1], r_halo.at[h, 0], device(z_next))
        acc[...] = jnp.zeros_like(acc)
        for e in range(1, QUAD - 1):
            wait(kv_slot(e + 1), r_kv.at[h, e])

        def query_slot(index, inner):
            half = index // 2
            first = (1 - index) * (1 - half) + (5 - index) * half
            i = first + p * (QUAD - 1 - 2 * first)
            wait(qob.at[h, :, slab(i)], r_qo.at[h, i])

            @pl.when(i == 0)
            def _():
                wait(kv_slot(0), r_halo.at[h, 0])

            @pl.when(i == QUAD - 1)
            def _():
                wait(kv_slot(QUAD + 1), r_halo.at[h, 1])

            attend(h, i)
            post(h, i, 0, 1, 0)

            @pl.when(i == 0)
            def _():
                hs[h, 0, 0] = (acc[0, 0:rows] * scale).astype(BF)
                hs[h, 0, 1] = acc[1, 0:rows].astype(BF)
                send(hs.at[h, 0], hr.at[h, 1], s_part.at[h, 0], r_part.at[h, 1], device(z_prev))

            @pl.when(i == QUAD - 1)
            def _():
                hs[h, 1, 0] = (acc[0, 5 * rows :] * scale).astype(BF)
                hs[h, 1, 1] = acc[1, 5 * rows :].astype(BF)
                send(hs.at[h, 1], hr.at[h, 0], s_part.at[h, 1], r_part.at[h, 0], device(z_next))

            return inner

        lax.fori_loop(0, QUAD, query_slot, 0)

        def finish(index, inner):
            half = index // 2
            first = (1 - index) * (1 - half) + index * half
            i = first + p * (QUAD - 1 - 2 * first)
            edge = (i == 0) | (i == QUAD - 1)
            side = i // (QUAD - 1)

            @pl.when(edge)
            def _():
                wait(hr.at[h, side], r_part.at[h, side])
                ob[h, i, 1] = (acc[0, slab(i + 1)] * scale + hr[h, side, 0].astype(F32)).astype(BF)
                ob[h, i, 2] = (acc[1, slab(i + 1)] + hr[h, side, 1].astype(F32)).astype(BF)

            @pl.when(jnp.logical_not(edge))
            def _():
                ob[h, i, 1] = (acc[0, slab(i + 1)] * scale).astype(BF)
                ob[h, i, 2] = acc[1, slab(i + 1)].astype(BF)

            post(h, i, 1, 2, 1)
            return inner

        lax.fori_loop(0, QUAD, finish, 0)

        @pl.when(h >= LAG)
        def _():
            relay(h - LAG)

        return carry

    lax.fori_loop(0, own, step, 0)

    def tail(h, carry):
        relay(h)
        return carry

    lax.fori_loop(max(own - LAG, 0), own, tail, 0)

    def drain(h, carry):
        wait(ob.at[h], s_in.at[h])
        wait(ob.at[h], s_out.at[h])
        wait(rl.at[h], s_rl.at[h])
        for e in range(2):
            wait(hs.at[h, e], s_halo.at[h, e])
            wait(hs.at[h, e], s_part.at[h, e])
        wait(ob.at[h], r_fin.at[h])
        return carry

    lax.fori_loop(0, own, drain, 0)
    for d in range(QUAD - 1):
        wait(adj_ref, s_b.at[d])


LAG = 3


def per_device(query, key, value, cotangent, adjacency, *, sections, shards):
    _, rows, width = query.shape
    own = width // HD // QUAD
    tiles, links = adjacency.shape
    tile = rows // tiles
    dma, vmem = pltpu.SemaphoreType.DMA, pltpu.VMEM
    hbm = pl.BlockSpec(memory_space=pltpu.HBM)
    out = pl.pallas_call(
        functools.partial(kernel, rows=rows, own=own, tile=tile, sections=sections, shards=shards),
        out_shape=pltpu.VMEM((3, rows, width), BF),
        in_specs=[hbm] * 5,
        out_specs=pl.BlockSpec(memory_space=pltpu.VMEM),
        scratch_shapes=[
            vmem((own, 2, (QUAD + 2) * rows, HD), BF),
            vmem((own, 2, QUAD * rows, HD), BF),
            vmem((QUAD, tiles, links), jnp.int32),
            vmem((QUAD, 16, rows), F32),
            vmem((own, QUAD, 3, rows, HD), BF),
            vmem((own, 2, 2, rows, HD), BF),
            vmem((own, 2, 2, rows, HD), BF),
            vmem((own, 2, 3, rows, HD), BF),
            vmem((2, (QUAD + 2) * rows, HD), F32),
            dma((own, QUAD)),
            dma((own, QUAD)),
            dma((QUAD,)),
            dma((own, 2)),
            dma((own, 2)),
            dma((own, 2, 2)),
            dma((own,)),
            dma((own,)),
            dma((QUAD - 1,)),
            dma((own, 2)),
            dma((own, 2)),
            dma((own,)),
            dma((own,)),
            pltpu.SemaphoreType.REGULAR,
            pltpu.SemaphoreType.REGULAR,
        ],
        compiler_params=pltpu.CompilerParams(
            collective_id=0, has_side_effects=True, vmem_limit_bytes=54 * 1024 * 1024
        ),
    )(query[0], key[0], value[0], cotangent[0], adjacency)
    return jnp.transpose(out, (1, 0, 2))[None]


def solution(mesh):
    in_specs = (
        P("section", "seq", None),
        P("section", "seq", None),
        P("section", "seq", None),
        P("section", "seq", None),
        P("seq", None),
    )
    out_specs = P("section", "seq", None, None)
    body = functools.partial(per_device, sections=mesh.shape["section"], shards=mesh.shape["seq"])
    return jax.shard_map(body, mesh=mesh, in_specs=in_specs, out_specs=out_specs, check_vma=False)
```

```python
import functools
import math

import jax
import jax.numpy as jnp
from jax import lax
from jax.experimental import pallas as pl
from jax.experimental.pallas import tpu as pltpu
from jax.sharding import PartitionSpec as P

HD = 128
QUAD = 4
NEG = -1e30
BF = jnp.bfloat16
F32 = jnp.float32


def dot(a, b, dims):
    return lax.dot_general(a, b, (dims, ((), ())), preferred_element_type=F32)


def kernel(
    q_ref, k_ref, v_ref, o_ref, adj_ref, out_ref,
    kvb, qob, adjb, biasb, ob, hs, hr, rl, acc,
    r_kv, r_qo, r_b, r_halo, r_part, r_rl, r_fin,
    s_in, s_b, s_halo, s_part, s_out, s_rl, quad_in, near_in,
    *, rows, own, tile, sections, shards,
):
    nz = shards // QUAD
    seq = lax.axis_index("seq")
    sec = lax.axis_index("section")
    z, g = seq // QUAD, seq % QUAD
    p, c = g // 2, g % 2
    base = z * QUAD
    target = (sec + sections - 1) % sections
    source = (sec + 1) % sections
    other = base + 2 * (1 - p)
    z_prev = ((z + nz - 1) % nz) * QUAD + g
    z_next = ((z + 1) % nz) * QUAD + g
    scale = HD**-0.5
    window = 3 * rows
    mesh_id = pl.DeviceIdType.MESH

    def device(at_seq, at_sec=None):
        return {"seq": at_seq, "section": sec if at_sec is None else at_sec}

    def cols(head):
        return pl.ds(pl.multiple_of(head * HD, HD), HD)

    def slab(slot):
        return pl.ds(pl.multiple_of(slot * rows, rows), rows)

    def send(src, dst, ssem, rsem, to):
        pltpu.make_async_remote_copy(
            src_ref=src, dst_ref=dst, send_sem=ssem, recv_sem=rsem, device_id=to, device_id_type=mesh_id
        ).start()

    def wait(ref, sem):
        pltpu.make_async_copy(ref, ref, sem).wait()

    barrier = pltpu.get_barrier_semaphore()
    for e in (1, 3):

        @pl.when(g != e)
        def _():
            pl.semaphore_signal(barrier, inc=1, device_id=device(base + e), device_id_type=mesh_id)

    @pl.when(c == 1)
    def _():
        pl.semaphore_wait(barrier, QUAD - 1)
        pl.semaphore_signal(quad_in, inc=1, device_id=device(base + g - 1), device_id_type=mesh_id)
        for to in (device(z_prev - 1), device(z_next - 1), device(seq - 1, target), device(seq - 1, source)):
            pl.semaphore_signal(barrier, inc=1, device_id=to, device_id_type=mesh_id)

    @pl.when(c == 0)
    def _():
        pl.semaphore_wait(quad_in, 1)

    for d in range(1, QUAD):
        to = device(base + (g + d) % QUAD)
        send(adj_ref, adjb.at[g], s_b.at[d - 1], r_b.at[g], to)
    pltpu.make_async_copy(adj_ref, adjb.at[g], r_b.at[g]).start()

    def scatter(h, carry):
        mine = cols(g * own + h)
        pltpu.make_async_copy(k_ref.at[:, mine], kvb.at[h, 0, slab(g + 1)], r_kv.at[h, g]).start()
        pltpu.make_async_copy(v_ref.at[:, mine], kvb.at[h, 1, slab(g + 1)], r_kv.at[h, g]).start()
        pltpu.make_async_copy(q_ref.at[:, mine], qob.at[h, 0, slab(g)], r_qo.at[h, g]).start()
        pltpu.make_async_copy(o_ref.at[:, mine], qob.at[h, 1, slab(g)], r_qo.at[h, g]).start()
        for peer in (2 * (1 - p), 2 * (1 - p) + 1, 2 * p + 1 - c):
            to = device(base + peer)
            theirs = cols(peer * own + h)
            send(k_ref.at[:, theirs], kvb.at[h, 0, slab(g + 1)], s_in.at[h], r_kv.at[h, g], to)
            send(v_ref.at[:, theirs], kvb.at[h, 1, slab(g + 1)], s_in.at[h], r_kv.at[h, g], to)
            send(q_ref.at[:, theirs], qob.at[h, 0, slab(g)], s_in.at[h], r_qo.at[h, g], to)
            send(o_ref.at[:, theirs], qob.at[h, 1, slab(g)], s_in.at[h], r_qo.at[h, g], to)
        return carry

    lax.fori_loop(0, own, scatter, 0)

    @pl.when(c == 0)
    def _():
        pl.semaphore_wait(barrier, 4)
        pl.semaphore_signal(near_in, inc=1, device_id=device(base + g + 1), device_id_type=mesh_id)

    @pl.when(c == 1)
    def _():
        pl.semaphore_wait(near_in, 1)

    def post(h, i, first, count, kind):
        to = device(other + i % 2, target)
        src = ob.at[h, i, pl.ds(first, count)]

        @pl.when(i // 2 != p)
        def _():
            send(src, out_ref.at[pl.ds(first, count), :, cols(g * own + h)], s_out.at[h], r_fin.at[h], to)

        @pl.when(i // 2 == p)
        def _():
            send(src, rl.at[h, c, pl.ds(first, count)], s_out.at[h], r_rl.at[h, c, kind], to)

    def relay(h):
        to = device(other + c)
        for kind, first, count in ((0, 0, 1), (1, 1, 2)):
            for e in range(2):
                block = rl.at[h, e, pl.ds(first, count)]
                wait(block, r_rl.at[h, e, kind])
                head = (2 * (1 - p) + e) * own + h
                send(block, out_ref.at[pl.ds(first, count), :, cols(head)], s_rl.at[h], r_fin.at[h], to)

    def attend(h, i):
        win = pl.ds(pl.multiple_of(i * rows, rows), window)
        keys, values = kvb[h, 0, win, :], kvb[h, 1, win, :]
        queries, grads = qob[h, 0, slab(i), :], qob[h, 1, slab(i), :]
        scores = dot(keys, queries, ((1,), (1,)))
        bias = biasb[i]
        count = window // tile
        scores = jnp.concatenate(
            [scores[j * tile : (j + 1) * tile] + bias[j : j + 1] for j in range(count)], axis=0
        )
        top = jnp.max(scores, axis=0, keepdims=True)
        weight = jnp.exp2((scores - top) * (scale * math.log2(math.e)))
        total = jnp.sum(weight, axis=0, keepdims=True)
        prob = weight * (1.0 / total)
        half = prob.astype(BF)
        dprob = dot(values, grads, ((1,), (1,)))
        delta = jnp.sum(half.astype(F32) * dprob, axis=0, keepdims=True)
        dscore = (prob * (dprob - delta)).astype(BF)
        ob[h, i, 0] = (dot(dscore, keys, ((0,), (0,))) * scale).astype(BF)
        acc[0, win, :] += dot(dscore, queries, ((1,), (0,)))
        acc[1, win, :] += dot(half, grads, ((1,), (0,)))

    for e in range(QUAD):
        wait(adj_ref, r_b.at[e])
        rule = adjb[e]
        for j in range(window // tile):
            for n in range(rows // tile):
                link = jnp.broadcast_to(rule[n : n + 1, j : j + 1], (1, tile))
                biasb[e, j : j + 1, n * tile : (n + 1) * tile] = jnp.where(link > 0, 0.0, NEG)

    def step(h, carry):
        kv_slot = lambda slot: kvb.at[h, :, slab(slot)]
        wait(kv_slot(1), r_kv.at[h, 0])
        send(kv_slot(1), kv_slot(QUAD + 1), s_halo.at[h, 0], r_halo.at[h, 1], device(z_prev))
        wait(kv_slot(QUAD), r_kv.at[h, QUAD - 1])
        send(kv_slot(QUAD), kv_slot(0), s_halo.at[h, 1], r_halo.at[h, 0], device(z_next))
        acc[...] = jnp.zeros_like(acc)
        for e in range(1, QUAD - 1):
            wait(kv_slot(e + 1), r_kv.at[h, e])

        def query_slot(index, inner):
            half = index // 2
            first = (1 - index) * (1 - half) + (5 - index) * half
            i = first + p * (QUAD - 1 - 2 * first)
            wait(qob.at[h, :, slab(i)], r_qo.at[h, i])

            @pl.when(i == 0)
            def _():
                wait(kv_slot(0), r_halo.at[h, 0])

            @pl.when(i == QUAD - 1)
            def _():
                wait(kv_slot(QUAD + 1), r_halo.at[h, 1])

            attend(h, i)
            post(h, i, 0, 1, 0)

            @pl.when(i == 0)
            def _():
                hs[h, 0, 0] = (acc[0, 0:rows] * scale).astype(BF)
                hs[h, 0, 1] = acc[1, 0:rows].astype(BF)
                send(hs.at[h, 0], hr.at[h, 1], s_part.at[h, 0], r_part.at[h, 1], device(z_prev))

            @pl.when(i == QUAD - 1)
            def _():
                hs[h, 1, 0] = (acc[0, 5 * rows :] * scale).astype(BF)
                hs[h, 1, 1] = acc[1, 5 * rows :].astype(BF)
                send(hs.at[h, 1], hr.at[h, 0], s_part.at[h, 1], r_part.at[h, 0], device(z_next))

            return inner

        lax.fori_loop(0, QUAD, query_slot, 0)

        def finish(index, inner):
            half = index // 2
            first = (1 - index) * (1 - half) + index * half
            i = first + p * (QUAD - 1 - 2 * first)
            edge = (i == 0) | (i == QUAD - 1)
            side = i // (QUAD - 1)

            @pl.when(edge)
            def _():
                wait(hr.at[h, side], r_part.at[h, side])
                ob[h, i, 1] = (acc[0, slab(i + 1)] * scale + hr[h, side, 0].astype(F32)).astype(BF)
                ob[h, i, 2] = (acc[1, slab(i + 1)] + hr[h, side, 1].astype(F32)).astype(BF)

            @pl.when(jnp.logical_not(edge))
            def _():
                ob[h, i, 1] = (acc[0, slab(i + 1)] * scale).astype(BF)
                ob[h, i, 2] = acc[1, slab(i + 1)].astype(BF)

            post(h, i, 1, 2, 1)
            return inner

        lax.fori_loop(0, QUAD, finish, 0)

        @pl.when(h >= LAG)
        def _():
            relay(h - LAG)

        return carry

    lax.fori_loop(0, own, step, 0)

    def tail(h, carry):
        relay(h)
        return carry

    lax.fori_loop(max(own - LAG, 0), own, tail, 0)

    def drain(h, carry):
        wait(ob.at[h], s_in.at[h])
        wait(ob.at[h], s_out.at[h])
        wait(rl.at[h], s_rl.at[h])
        for e in range(2):
            wait(hs.at[h, e], s_halo.at[h, e])
            wait(hs.at[h, e], s_part.at[h, e])
        wait(ob.at[h], r_fin.at[h])
        return carry

    lax.fori_loop(0, own, drain, 0)
    for d in range(QUAD - 1):
        wait(adj_ref, s_b.at[d])


LAG = 3


def per_device(query, key, value, cotangent, adjacency, *, sections, shards):
    _, rows, width = query.shape
    own = width // HD // QUAD
    tiles, links = adjacency.shape
    tile = rows // tiles
    dma, vmem = pltpu.SemaphoreType.DMA, pltpu.VMEM
    hbm = pl.BlockSpec(memory_space=pltpu.HBM)
    out = pl.pallas_call(
        functools.partial(kernel, rows=rows, own=own, tile=tile, sections=sections, shards=shards),
        out_shape=pltpu.VMEM((3, rows, width), BF),
        in_specs=[hbm] * 5,
        out_specs=pl.BlockSpec(memory_space=pltpu.VMEM),
        scratch_shapes=[
            vmem((own, 2, (QUAD + 2) * rows, HD), BF),
            vmem((own, 2, QUAD * rows, HD), BF),
            vmem((QUAD, tiles, links), jnp.int32),
            vmem((QUAD, 16, rows), F32),
            vmem((own, QUAD, 3, rows, HD), BF),
            vmem((own, 2, 2, rows, HD), BF),
            vmem((own, 2, 2, rows, HD), BF),
            vmem((own, 2, 3, rows, HD), BF),
            vmem((2, (QUAD + 2) * rows, HD), F32),
            dma((own, QUAD)),
            dma((own, QUAD)),
            dma((QUAD,)),
            dma((own, 2)),
            dma((own, 2)),
            dma((own, 2, 2)),
            dma((own,)),
            dma((own,)),
            dma((QUAD - 1,)),
            dma((own, 2)),
            dma((own, 2)),
            dma((own,)),
            dma((own,)),
            pltpu.SemaphoreType.REGULAR,
            pltpu.SemaphoreType.REGULAR,
        ],
        compiler_params=pltpu.CompilerParams(
            collective_id=0, has_side_effects=True, vmem_limit_bytes=54 * 1024 * 1024
        ),
    )(query[0], key[0], value[0], cotangent[0], adjacency)
    return jnp.transpose(out, (1, 0, 2))[None]


def solution(mesh):
    in_specs = (
        P("section", "seq", None),
        P("section", "seq", None),
        P("section", "seq", None),
        P("section", "seq", None),
        P("seq", None),
    )
    out_specs = P("section", "seq", None, None)
    body = functools.partial(per_device, sections=mesh.shape["section"], shards=mesh.shape["seq"])
    return jax.shard_map(body, mesh=mesh, in_specs=in_specs, out_specs=out_specs, check_vma=False)
```

```python
import functools
import math

import jax
import jax.numpy as jnp
from jax import lax
from jax.experimental import pallas as pl
from jax.experimental.pallas import tpu as pltpu
from jax.sharding import PartitionSpec as P

HD = 128
QUAD = 4
NEG = -1e30
BF = jnp.bfloat16
F32 = jnp.float32


def dot(a, b, dims):
    return lax.dot_general(a, b, (dims, ((), ())), preferred_element_type=F32)


def kernel(
    q_ref, k_ref, v_ref, o_ref, adj_ref, out_ref,
    kvb, qob, adjb, biasb, ob, hs, hr, rl, acc,
    r_kv, r_qo, r_b, r_halo, r_part, r_rl, r_fin,
    s_in, s_b, s_halo, s_part, s_out, s_rl, quad_in, near_in,
    *, rows, own, tile, sections, shards,
):
    nz = shards // QUAD
    seq = lax.axis_index("seq")
    sec = lax.axis_index("section")
    z, g = seq // QUAD, seq % QUAD
    p, c = g // 2, g % 2
    base = z * QUAD
    target = (sec + sections - 1) % sections
    source = (sec + 1) % sections
    other = base + 2 * (1 - p)
    z_prev = ((z + nz - 1) % nz) * QUAD + g
    z_next = ((z + 1) % nz) * QUAD + g
    scale = HD**-0.5
    window = 3 * rows
    mesh_id = pl.DeviceIdType.MESH

    def device(at_seq, at_sec=None):
        return {"seq": at_seq, "section": sec if at_sec is None else at_sec}

    def cols(head):
        return pl.ds(pl.multiple_of(head * HD, HD), HD)

    def slab(slot):
        return pl.ds(pl.multiple_of(slot * rows, rows), rows)

    def send(src, dst, ssem, rsem, to):
        pltpu.make_async_remote_copy(
            src_ref=src, dst_ref=dst, send_sem=ssem, recv_sem=rsem, device_id=to, device_id_type=mesh_id
        ).start()

    def wait(ref, sem):
        pltpu.make_async_copy(ref, ref, sem).wait()

    barrier = pltpu.get_barrier_semaphore()
    for e in (1, 3):

        @pl.when(g != e)
        def _():
            pl.semaphore_signal(barrier, inc=1, device_id=device(base + e), device_id_type=mesh_id)

    @pl.when(c == 1)
    def _():
        pl.semaphore_wait(barrier, QUAD - 1)
        pl.semaphore_signal(quad_in, inc=1, device_id=device(base + g - 1), device_id_type=mesh_id)

    @pl.when(c == 0)
    def _():
        pl.semaphore_wait(quad_in, 1)

    for d in range(1, QUAD):
        to = device(base + (g + d) % QUAD)
        send(adj_ref, adjb.at[g], s_b, r_b, to)
    pltpu.make_async_copy(adj_ref, adjb.at[g], r_b).start()

    def scatter(h, carry):
        for peer in (2 * (1 - p), 2 * (1 - p) + 1, 2 * p + 1 - c):
            to = device(base + peer)
            theirs = cols(peer * own + h)
            send(k_ref.at[:, theirs], kvb.at[h, 0, slab(g + 1)], s_in.at[h // 2], r_kv.at[h, p], to)
            send(v_ref.at[:, theirs], kvb.at[h, 1, slab(g + 1)], s_in.at[h // 2], r_kv.at[h, p], to)
            send(q_ref.at[:, theirs], qob.at[h, 0, slab(g)], s_in.at[h // 2], r_qo.at[h, p], to)
            send(o_ref.at[:, theirs], qob.at[h, 1, slab(g)], s_in.at[h // 2], r_qo.at[h, p], to)
        mine = cols(g * own + h)
        pltpu.make_async_copy(k_ref.at[:, mine], kvb.at[h, 0, slab(g + 1)], r_kv.at[h, p]).start()
        pltpu.make_async_copy(v_ref.at[:, mine], kvb.at[h, 1, slab(g + 1)], r_kv.at[h, p]).start()
        pltpu.make_async_copy(q_ref.at[:, mine], qob.at[h, 0, slab(g)], r_qo.at[h, p]).start()
        pltpu.make_async_copy(o_ref.at[:, mine], qob.at[h, 1, slab(g)], r_qo.at[h, p]).start()
        return carry

    lax.fori_loop(0, own, scatter, 0)

    @pl.when(c == 1)
    def _():
        for to in (device(z_prev - 1), device(z_next - 1), device(seq - 1, target), device(seq - 1, source)):
            pl.semaphore_signal(barrier, inc=1, device_id=to, device_id_type=mesh_id)

    @pl.when(c == 0)
    def _():
        pl.semaphore_wait(barrier, 4)
        pl.semaphore_signal(near_in, inc=1, device_id=device(base + g + 1), device_id_type=mesh_id)

    @pl.when(c == 1)
    def _():
        pl.semaphore_wait(near_in, 1)

    def post(h, i, first, count, kind):
        to = device(other + i % 2, target)
        src = ob.at[h, i, pl.ds(first, count)]

        @pl.when(i // 2 != p)
        def _():
            send(src, out_ref.at[pl.ds(first, count), :, cols(g * own + h)], s_out.at[h // 2], r_fin.at[h // 2], to)

        @pl.when(i // 2 == p)
        def _():
            send(src, rl.at[h, c, pl.ds(first, count)], s_out.at[h // 2], r_rl.at[h, kind], to)

    def relay(h):
        to = device(other + c)
        for kind, first, count in ((0, 0, 1), (1, 1, 2)):
            wait(rl.at[h, :, pl.ds(first, count)], r_rl.at[h, kind])
            for e in range(2):
                block = rl.at[h, e, pl.ds(first, count)]
                head = (2 * (1 - p) + e) * own + h
                send(block, out_ref.at[pl.ds(first, count), :, cols(head)], s_rl.at[h // 2], r_fin.at[h // 2], to)

    def attend(h, i):
        win = pl.ds(pl.multiple_of(i * rows, rows), window)
        keys, values = kvb[h, 0, win, :], kvb[h, 1, win, :]
        queries, grads = qob[h, 0, slab(i), :], qob[h, 1, slab(i), :]
        scores = dot(keys, queries, ((1,), (1,)))
        bias = biasb[i]
        count = window // tile
        scores = jnp.concatenate(
            [scores[j * tile : (j + 1) * tile] + bias[j : j + 1] for j in range(count)], axis=0
        )
        top = jnp.max(scores, axis=0, keepdims=True)
        weight = jnp.exp2((scores - top) * (scale * math.log2(math.e)))
        total = jnp.sum(weight, axis=0, keepdims=True)
        prob = weight * (1.0 / total)
        half = prob.astype(BF)
        dprob = dot(values, grads, ((1,), (1,)))
        delta = jnp.sum(half.astype(F32) * dprob, axis=0, keepdims=True)
        dscore = (prob * (dprob - delta)).astype(BF)
        ob[h, i, 0] = (dot(dscore, keys, ((0,), (0,))) * scale).astype(BF)
        acc[0, win, :] += dot(dscore, queries, ((1,), (0,)))
        acc[1, win, :] += dot(half, grads, ((1,), (0,)))

    wait(adjb, r_b)
    for e in range(QUAD):
        rule = adjb[e]
        for j in range(window // tile):
            for n in range(rows // tile):
                link = jnp.broadcast_to(rule[n : n + 1, j : j + 1], (1, tile))
                biasb[e, j : j + 1, n * tile : (n + 1) * tile] = jnp.where(link > 0, 0.0, NEG)

    def step(h, carry):
        kv_slot = lambda slot: kvb.at[h, :, slab(slot)]
        wait(kvb.at[h, :, pl.ds(rows, 2 * rows)], r_kv.at[h, 0])
        send(kv_slot(1), kv_slot(QUAD + 1), s_halo, r_halo.at[h], device(z_prev))
        wait(kvb.at[h, :, pl.ds(3 * rows, 2 * rows)], r_kv.at[h, 1])
        send(kv_slot(QUAD), kv_slot(0), s_halo, r_halo.at[h], device(z_next))
        acc[...] = jnp.zeros_like(acc)

        def query_slot(index, inner):
            half = index // 2
            first = (1 - index) * (1 - half) + (5 - index) * half
            i = first + p * (QUAD - 1 - 2 * first)
            side = half + p * (1 - 2 * half)

            @pl.when(index % 2 == 0)
            def _():
                wait(qob.at[h, :, pl.ds(pl.multiple_of(side * 2 * rows, 2 * rows), 2 * rows)], r_qo.at[h, side])

            @pl.when(index == 1)
            def _():
                wait(kvb.at[h, :, pl.ds(0, 2 * rows)], r_halo.at[h])

            attend(h, i)
            post(h, i, 0, 1, 0)

            @pl.when(i == 0)
            def _():
                hs[h, 0, 0] = (acc[0, 0:rows] * scale).astype(BF)
                hs[h, 0, 1] = acc[1, 0:rows].astype(BF)
                send(hs.at[h, 0], hr.at[h, 1], s_part, r_part.at[h], device(z_prev))

            @pl.when(i == QUAD - 1)
            def _():
                hs[h, 1, 0] = (acc[0, 5 * rows :] * scale).astype(BF)
                hs[h, 1, 1] = acc[1, 5 * rows :].astype(BF)
                send(hs.at[h, 1], hr.at[h, 0], s_part, r_part.at[h], device(z_next))

            return inner

        lax.fori_loop(0, QUAD, query_slot, 0)

        wait(hr.at[h], r_part.at[h])

        def finish(index, inner):
            half = index // 2
            first = (1 - index) * (1 - half) + index * half
            i = first + p * (QUAD - 1 - 2 * first)
            edge = (i == 0) | (i == QUAD - 1)
            side = i // (QUAD - 1)

            @pl.when(edge)
            def _():
                ob[h, i, 1] = (acc[0, slab(i + 1)] * scale + hr[h, side, 0].astype(F32)).astype(BF)
                ob[h, i, 2] = (acc[1, slab(i + 1)] + hr[h, side, 1].astype(F32)).astype(BF)

            @pl.when(jnp.logical_not(edge))
            def _():
                ob[h, i, 1] = (acc[0, slab(i + 1)] * scale).astype(BF)
                ob[h, i, 2] = acc[1, slab(i + 1)].astype(BF)

            post(h, i, 1, 2, 1)
            return inner

        lax.fori_loop(0, QUAD, finish, 0)

        @pl.when(h >= LAG)
        def _():
            relay(h - LAG)

        return carry

    lax.fori_loop(0, own, step, 0)

    def tail(h, carry):
        relay(h)
        return carry

    lax.fori_loop(max(own - LAG, 0), own, tail, 0)

    wait(hs, s_halo)
    wait(hs, s_part)
    wait(adjb.at[pl.ds(0, QUAD - 1)], s_b)

    def drain(pair, carry):
        heads = pl.ds(2 * pair, 2)
        wait(ob.at[heads], s_in.at[pair])
        wait(ob.at[heads], s_out.at[pair])
        wait(rl.at[heads], s_rl.at[pair])
        wait(ob.at[heads], r_fin.at[pair])
        return carry

    lax.fori_loop(0, own // 2, drain, 0)


LAG = 3


def per_device(query, key, value, cotangent, adjacency, *, sections, shards):
    _, rows, width = query.shape
    own = width // HD // QUAD
    tiles, links = adjacency.shape
    tile = rows // tiles
    dma, vmem = pltpu.SemaphoreType.DMA, pltpu.VMEM
    hbm = pl.BlockSpec(memory_space=pltpu.HBM)
    out = pl.pallas_call(
        functools.partial(kernel, rows=rows, own=own, tile=tile, sections=sections, shards=shards),
        out_shape=pltpu.VMEM((3, rows, width), BF),
        in_specs=[hbm] * 5,
        out_specs=pl.BlockSpec(memory_space=pltpu.VMEM),
        scratch_shapes=[
            vmem((own, 2, (QUAD + 2) * rows, HD), BF),
            vmem((own, 2, QUAD * rows, HD), BF),
            vmem((QUAD, tiles, links), jnp.int32),
            vmem((QUAD, 16, rows), F32),
            vmem((own, QUAD, 3, rows, HD), BF),
            vmem((own, 2, 2, rows, HD), BF),
            vmem((own, 2, 2, rows, HD), BF),
            vmem((own, 2, 3, rows, HD), BF),
            vmem((2, (QUAD + 2) * rows, HD), F32),
            dma((own, 2)),
            dma((own, 2)),
            dma,
            dma((own,)),
            dma((own,)),
            dma((own, 2)),
            dma((own // 2,)),
            dma((own // 2,)),
            dma,
            dma,
            dma,
            dma((own // 2,)),
            dma((own // 2,)),
            pltpu.SemaphoreType.REGULAR,
            pltpu.SemaphoreType.REGULAR,
        ],
        compiler_params=pltpu.CompilerParams(
            collective_id=0, has_side_effects=True, vmem_limit_bytes=54 * 1024 * 1024
        ),
    )(query[0], key[0], value[0], cotangent[0], adjacency)
    return jnp.transpose(out, (1, 0, 2))[None]


def solution(mesh):
    in_specs = (
        P("section", "seq", None),
        P("section", "seq", None),
        P("section", "seq", None),
        P("section", "seq", None),
        P("seq", None),
    )
    out_specs = P("section", "seq", None, None)
    body = functools.partial(per_device, sections=mesh.shape["section"], shards=mesh.shape["seq"])
    return jax.shard_map(body, mesh=mesh, in_specs=in_specs, out_specs=out_specs, check_vma=False)
```
